32 devices in a mesh: expert: 16 (over z, y, x), tok: 2 (over core).
Axes of the slice: x: 2, y: 2, z: 4, core: 2. Of those that a mesh axis runs over, the one named last changes fastest.
Arguments:
- tokens: bfloat16 [2048, 3584], P(('expert', 'tok')), may hold values from -6 to 6
- routes: int32 [2048, 8], P(('expert', 'tok')), may hold values from 0 to 15, all different within a row; in each aligned block of 64 rows (0 to 63, 64 to 127, ...) at most 36 rows name the same one
- gates: float32 [2048, 8], P(('expert', 'tok')), may hold values from 0.05 to 1
- upstream: bfloat16 [2048, 3584], P(('expert', 'tok')), may hold values from -6 to 6
- w_up: bfloat16 [16, 3584, 1024], P('expert', None, 'tok'), may hold values from -0.09375 to 0.09375
- w_down: bfloat16 [16, 1024, 3584], P('expert', 'tok'), may hold values from -0.1875 to 0.1875
Outputs:
- mixed: bfloat16 [2048, 3584], P(('expert', 'tok'))
- d_tokens: bfloat16 [2048, 3584], P(('expert', 'tok'))
- d_gates: float32 [2048, 8], P(('expert', 'tok'))
- grad_up: bfloat16 [16, 3584, 1024], P('expert', None, 'tok')
- grad_down: bfloat16 [16, 1024, 3584], P('expert', 'tok')
The draws below stay inside these ranges and needn't reach their ends.
Inputs may be any that keep to these rules, and one draw needn't show every extreme that they name: `routes`: each token names 8 different experts. At most 36 of the 64 tokens of one device name the same expert, and in every draw the tokens of some device name some expert exactly 36 times.
All inputs are finite; a program needn't handle non-finite values.
Results may differ from the reference program's by a relative error of at most 0.0065.
Values may be sent and summed in bfloat16 or wider, within the bound.
A program may use at most 192 MiB of HBM per device.

```python
import math
import jax
import jax.numpy as jnp
import numpy as np
from jax import lax

D = 3584
HID = 1024
TOP = 8
TOK_DEV = 64
EXPERTS = 16
TOKENS = 2048
CAP = 36
SLOTS = 1152


def steps_of(rng, dims, pieces, least, top_value):
    factor_of, own = 1.0, jax.random.fold_in(rng, 6)
    for dim, parts in pieces:
        draws = jnp.exp(jax.random.uniform(jax.random.fold_in(own, dim), (parts,), jnp.float32, least / len(pieces), top_value / len(pieces)))
        factor_of = factor_of * jnp.repeat(draws, dims[dim] // parts).reshape([-1 if axis == dim else 1 for axis in range(len(dims))])
    return factor_of


def routed_block(rng, own, number, rows, number_of, top, bound, lean):
    order = jax.random.permutation(rng, number_of)
    packed, common = shares(number_of, rows * top, bound, lean, True), shares(number_of, rows * top, bound, lean, False)
    places = jnp.arange(number_of)

    def named(tallies, turn):
        used = int((tallies > 0).sum())
        fixed = max(1, used // 4)
        passed = fixed + (places - fixed + turn * (used - fixed)) % max(1, number_of - fixed)
        return jnp.zeros((number_of,), jnp.int32).at[order[jnp.where(places < fixed, places, passed)]].set(jnp.asarray(tallies, jnp.int32))

    tallies = jnp.where(number % 4 == 0, named(packed, number // 4), named(common, number - number // 4 - 1))
    mixed = jax.random.permutation(jax.random.fold_in(own, 3), number_of)
    donor, receiver = mixed[0:number_of // 2 * 2:2], mixed[1:number_of // 2 * 2:2]
    slack = jnp.minimum(tallies[donor] - 1, bound - tallies[receiver]) // 2
    slack = jnp.where((donor == order[0]) | (receiver == order[0]) | (tallies[receiver] == 0), 0, jnp.maximum(slack, 0))
    passed = jax.random.randint(jax.random.fold_in(own, 4), (number_of // 2,), 0, 1 << 20) % (slack + 1)
    tallies = tallies.at[donor].add(-passed).at[receiver].add(passed)
    items = jnp.searchsorted(jnp.cumsum(tallies), jnp.arange(rows * top), side="right").astype(jnp.int32)
    grid = items.reshape(top, rows).T
    grid = grid[jax.random.permutation(jax.random.fold_in(own, 1), rows)]
    turn = jax.random.randint(jax.random.fold_in(own, 2), (rows, 1), 0, top)
    return jnp.take_along_axis(grid, (jnp.arange(top)[None, :] + turn) % top, axis=1)


def shares(count, total, reach, lean, full):
    weights = [(1 << 20) // math.isqrt(grade ** lean) + 1 for grade in range(1, count + 1)]
    largest = reach if full else min(reach, max(-(-total // count), total * weights[0] // sum(weights)))
    least = 1 if total - largest >= count - 1 else 0
    given, spare = [largest] + [least] * (count - 1), total - largest - least * (count - 1)
    while spare > 0:
        free = [i for i in range(1, count) if given[i] < largest] or [i for i in range(1, count) if given[i] < reach]
        whole, remaining = sum([weights[i] for i in free]), spare
        for i in free:
            extra = min(reach - given[i], max(1, remaining * weights[i] // whole), spare)
            given[i] = given[i] + extra
            spare = spare - extra
    return np.array(given)


def scatter_about(own_key, extent, width, reach, cuts=(), held_as=jnp.bfloat16):
    gain = steps_of(own_key, extent, cuts, -0.22, 0.18) if cuts else 1.0
    result = jax.random.normal(own_key, extent, jnp.float32) * width * gain
    return jnp.minimum(jnp.maximum(result, -reach), reach).astype(held_as)


def setup_inputs(seed: int = 0) -> dict:
    key_list = jax.random.split(jax.random.key(seed), 7)
    tokens = scatter_about(key_list[0], (TOKENS, D), 1.0, 6.0, ((0, 32),))
    routes_keys = jax.random.split(jax.random.fold_in(key_list[1], 1), TOKENS // TOK_DEV)
    routes_turns = jax.random.permutation(jax.random.fold_in(key_list[1], 3), TOKENS // TOK_DEV)
    routes = jax.vmap(lambda own, number: routed_block(jax.random.fold_in(key_list[1], 2), own, number, TOK_DEV, EXPERTS, TOP, CAP, 2))(routes_keys, routes_turns).reshape((TOKENS, TOP))
    gates = jnp.clip(jnp.exp(math.log(1.0) - 2.9957323 * jax.random.uniform(key_list[2], (TOKENS, TOP), jnp.float32) ** steps_of(key_list[2], (TOKENS, TOP), ((0, 32),), -0.2, 0.2)), 0.05, 1.0)
    upstream = scatter_about(key_list[3], (TOKENS, D), 1.0, 6.0, ((0, 32),))
    w_up = scatter_about(key_list[4], (EXPERTS, D, HID), D ** -0.5, 0.09375, ((0, 16), (2, 2)))
    w_down = scatter_about(key_list[5], (EXPERTS, HID, D), HID ** -0.5, 0.1875, ((0, 16), (1, 2)))
    return dict(tokens=tokens, routes=routes, gates=gates, upstream=upstream, w_up=w_up, w_down=w_down)


GELU_C = 0.7978845608028654
GELU_A = 0.044715


def gelu_value(hidden):
    inner_arg = GELU_C * (hidden + GELU_A * hidden * hidden * hidden)
    return 0.5 * hidden * (1.0 + jnp.tanh(inner_arg))


def gelu_slope(hidden):
    tangent = jnp.tanh(GELU_C * (hidden + GELU_A * hidden * hidden * hidden))
    return 0.5 * (1.0 + tangent) + 0.5 * hidden * (1.0 - tangent * tangent) * GELU_C * (1.0 + 3.0 * GELU_A * hidden * hidden)


def expert_rows(rows_x, rows_grad, up_local, down_local):
    hidden = jnp.dot(rows_x, up_local, preferred_element_type=jnp.float32)
    active = gelu_value(hidden).astype(jnp.bfloat16)
    out_part = jnp.dot(active, down_local, preferred_element_type=jnp.float32)
    d_active = lax.dot_general(rows_grad, down_local, (((1,), (1,)), ((), ())), preferred_element_type=jnp.float32)
    d_hidden = (d_active * gelu_slope(hidden)).astype(jnp.bfloat16)
    dx_part = lax.dot_general(d_hidden, up_local, (((1,), (1,)), ((), ())), preferred_element_type=jnp.float32)
    grad_down = lax.dot_general(active, rows_grad, (((0,), (0,)), ((), ())), preferred_element_type=jnp.float32)
    grad_up = lax.dot_general(rows_x, d_hidden, (((0,), (0,)), ((), ())), preferred_element_type=jnp.float32)
    return out_part, dx_part, grad_up, grad_down


def reference(tokens, routes, gates, upstream, w_up, w_down):
    assigned = routes.reshape(-1).astype(jnp.int32)
    sorted_order = jnp.argsort(assigned, stable=True).astype(jnp.int32)
    labels = jnp.arange(EXPERTS, dtype=jnp.int32)
    counts = jnp.sum((assigned[:, None] == labels[None, :]).astype(jnp.int32), axis=0).astype(jnp.int32)
    starts = (jnp.cumsum(counts) - counts).astype(jnp.int32)
    padded_order = jnp.concatenate([sorted_order, jnp.zeros((SLOTS,), jnp.int32)])
    gate_flat = gates.reshape(-1)
    positions = jnp.arange(SLOTS, dtype=jnp.int32)
    upstream_wide = upstream.astype(jnp.float32)

    def per_expert(state_now, expert):
        mixed_acc, dx_acc, dgate_acc = state_now
        picked_rows = lax.dynamic_slice_in_dim(padded_order, starts[expert], SLOTS).astype(jnp.int32)
        is_valid = positions < counts[expert]
        token_ids = (picked_rows // TOP).astype(jnp.int32)
        rows_x = jnp.where(is_valid[:, None], tokens[token_ids], jnp.zeros((), tokens.dtype))
        gate_rows = jnp.where(is_valid, gate_flat[picked_rows], jnp.zeros((), gates.dtype))
        rows_grad = (gate_rows[:, None] * upstream_wide[token_ids]).astype(jnp.bfloat16)
        out_part, dx_part, grad_up, grad_down = expert_rows(rows_x, rows_grad, w_up[expert], w_down[expert])
        out_rows = lax.optimization_barrier(out_part.astype(jnp.bfloat16)).astype(jnp.float32)
        dx_rows = lax.optimization_barrier(dx_part.astype(jnp.bfloat16)).astype(jnp.float32)
        mixed_acc = mixed_acc.at[token_ids].add(gate_rows[:, None] * out_rows)
        dx_acc = dx_acc.at[token_ids].add(jnp.where(is_valid[:, None], dx_rows, jnp.zeros((), dx_rows.dtype)))
        inner_sum = jnp.sum(upstream_wide[token_ids] * out_rows, axis=1)
        dgate_acc = dgate_acc.at[picked_rows].add(jnp.where(is_valid, inner_sum, jnp.zeros((), inner_sum.dtype)))
        return (mixed_acc, dx_acc, dgate_acc), (grad_up.astype(jnp.bfloat16), grad_down.astype(jnp.bfloat16))

    start_state = (jnp.zeros((TOKENS, D), jnp.float32), jnp.zeros((TOKENS, D), jnp.float32), jnp.zeros((TOKENS * TOP,), jnp.float32))
    final_state, grads = lax.scan(per_expert, start_state, jnp.arange(EXPERTS, dtype=jnp.int32))
    mixed_acc, dx_acc, dgate_acc = final_state
    grad_up, grad_down = grads
    return (mixed_acc.astype(jnp.bfloat16), dx_acc.astype(jnp.bfloat16), dgate_acc.reshape(TOKENS, TOP), grad_up, grad_down)
```

```python
import jax
import jax.numpy as jnp
from jax import lax
from jax.sharding import PartitionSpec as P

GELU_C = 0.7978845608028654
GELU_A = 0.044715


def gelu_value(hidden):
    inner_arg = GELU_C * (hidden + GELU_A * hidden * hidden * hidden)
    return 0.5 * hidden * (1.0 + jnp.tanh(inner_arg))


def gelu_slope(hidden):
    tangent = jnp.tanh(GELU_C * (hidden + GELU_A * hidden * hidden * hidden))
    return 0.5 * (1.0 + tangent) + 0.5 * hidden * (1.0 - tangent * tangent) * GELU_C * (
        1.0 + 3.0 * GELU_A * hidden * hidden
    )


def expert_rows(rows_x, rows_grad, up_local, down_local):
    hidden = jnp.dot(rows_x, up_local, preferred_element_type=jnp.float32)
    active = gelu_value(hidden).astype(jnp.bfloat16)
    out_part = jnp.dot(active, down_local, preferred_element_type=jnp.float32)
    d_active = lax.dot_general(
        rows_grad, down_local, (((1,), (1,)), ((), ())), preferred_element_type=jnp.float32
    )
    d_hidden = (d_active * gelu_slope(hidden)).astype(jnp.bfloat16)
    dx_part = lax.dot_general(
        d_hidden, up_local, (((1,), (1,)), ((), ())), preferred_element_type=jnp.float32
    )
    grad_down = lax.dot_general(
        active, rows_grad, (((0,), (0,)), ((), ())), preferred_element_type=jnp.float32
    )
    grad_up = lax.dot_general(
        rows_x, d_hidden, (((0,), (0,)), ((), ())), preferred_element_type=jnp.float32
    )
    return (out_part, dx_part, grad_up, grad_down)


def routed_shards(tokens, routes, gates, upstream, w_up, w_down):
    tok_rows, feature_width = tokens.shape
    top_count = routes.shape[1]
    owners = lax.axis_size("expert")
    pair_count = lax.axis_size("tok")
    capacity = tok_rows * top_count // owners + max(1, tok_rows * top_count // (8 * owners))
    assigned = routes.reshape(-1)
    labels = jnp.arange(owners, dtype=jnp.int32)
    onehot = (assigned[:, None] == labels[None, :]).astype(jnp.int32)
    earlier = jnp.cumsum(onehot, axis=0) - onehot
    slot_rank = jnp.sum(earlier * onehot, axis=1)
    slot_of = assigned * capacity + slot_rank
    slot_ids = jnp.arange(owners * capacity, dtype=jnp.int32)
    matches = (slot_of[None, :] == slot_ids[:, None]).astype(jnp.int32)
    filled = jnp.sum(matches, axis=1) > 0
    source = jnp.sum(matches * jnp.arange(assigned.shape[0], dtype=jnp.int32)[None, :], axis=1)
    token_ids = source // top_count
    send_x = jnp.where(filled[:, None], tokens[token_ids], jnp.zeros((), jnp.bfloat16))
    gate_rows = jnp.where(filled, gates.reshape(-1)[source], jnp.zeros((), jnp.float32))
    send_grad = (gate_rows[:, None] * upstream[token_ids].astype(jnp.float32)).astype(jnp.bfloat16)
    send_x = send_x.reshape(owners, capacity, feature_width)
    send_grad = send_grad.reshape(owners, capacity, feature_width)
    recv_x, recv_grad = (
        lax.all_to_all(send_x, "expert", split_axis=0, concat_axis=0, tiled=True),
        lax.all_to_all(send_grad, "expert", split_axis=0, concat_axis=0, tiled=True),
    )
    both_x, both_grad = (
        lax.all_gather(recv_x[None], "tok", axis=0, tiled=True),
        lax.all_gather(recv_grad[None], "tok", axis=0, tiled=True),
    )
    rows_x = both_x.reshape(-1, feature_width)
    rows_grad = both_grad.reshape(-1, feature_width)
    out_part, dx_part, grad_up, grad_down = expert_rows(rows_x, rows_grad, w_up[0], w_down[0])
    shaped_out = out_part.reshape(pair_count, owners, capacity, feature_width)
    shaped_dx = dx_part.reshape(pair_count, owners, capacity, feature_width)
    summed_out, summed_dx = (
        lax.psum_scatter(shaped_out, "tok", scatter_dimension=0, tiled=True),
        lax.psum_scatter(shaped_dx, "tok", scatter_dimension=0, tiled=True),
    )
    home_out, home_dx = (
        lax.all_to_all(
            summed_out[0].astype(jnp.bfloat16), "expert", split_axis=0, concat_axis=0, tiled=True
        ),
        lax.all_to_all(
            summed_dx[0].astype(jnp.bfloat16), "expert", split_axis=0, concat_axis=0, tiled=True
        ),
    )
    out_pairs = (
        home_out.reshape(owners * capacity, feature_width)[slot_of]
        .reshape(tok_rows, top_count, feature_width)
        .astype(jnp.float32)
    )
    dx_pairs = (
        home_dx.reshape(owners * capacity, feature_width)[slot_of]
        .reshape(tok_rows, top_count, feature_width)
        .astype(jnp.float32)
    )
    mixed_out = jnp.sum(gates[:, :, None] * out_pairs, axis=1).astype(jnp.bfloat16)
    d_gates = jnp.sum(upstream.astype(jnp.float32)[:, None, :] * out_pairs, axis=2)
    d_tokens = jnp.sum(dx_pairs, axis=1).astype(jnp.bfloat16)
    return (
        mixed_out,
        d_tokens,
        d_gates,
        grad_up.astype(jnp.bfloat16)[None],
        grad_down.astype(jnp.bfloat16)[None],
    )


def dense_shards(tokens, routes, gates, upstream, w_up, w_down):
    tok_rows, width = tokens.shape
    owners = lax.axis_size("expert")
    half = w_up.shape[2]
    swap = ((0, 1), (1, 0))
    up_local, down_local = w_up[0], w_down[0]
    up_full = jnp.concatenate([up_local, lax.ppermute(up_local, "tok", swap)], axis=1)
    down_full = jnp.concatenate([down_local, lax.ppermute(down_local, "tok", swap)], axis=0)
    named = routes[:, :, None] == jnp.arange(owners, dtype=jnp.int32)
    gate_of = jnp.sum(jnp.where(named, gates[:, :, None], 0.0), axis=1)
    gate = lax.all_to_all(gate_of.T, "expert", split_axis=0, concat_axis=0, tiled=True)
    gate = gate.reshape(-1)[:, None]
    all_x = lax.all_gather(tokens, "expert", axis=0, tiled=True)
    all_u = lax.all_gather(upstream, "expert", axis=0, tiled=True)
    hidden = jnp.dot(all_x, up_full, preferred_element_type=jnp.float32)
    gated = (gate * gelu_value(hidden)).astype(jnp.bfloat16)
    mixed_part = jnp.dot(gated, down_full, preferred_element_type=jnp.float32)
    mixed = lax.psum_scatter(
        mixed_part.astype(jnp.bfloat16), "expert", scatter_dimension=0, tiled=True
    )
    back = lax.dot_general(
        all_u, down_full, (((1,), (1,)), ((), ())), preferred_element_type=jnp.float32
    )
    inner = jnp.sum(gelu_value(hidden) * back, axis=1)
    d_hidden = (gate * back * gelu_slope(hidden)).astype(jnp.bfloat16)
    dx_part = lax.dot_general(
        d_hidden, up_full, (((1,), (1,)), ((), ())), preferred_element_type=jnp.float32
    )
    d_tokens = lax.psum_scatter(
        dx_part.astype(jnp.bfloat16), "expert", scatter_dimension=0, tiled=True
    )
    home = lax.all_to_all(
        inner.reshape(owners, tok_rows), "expert", split_axis=0, concat_axis=0, tiled=True
    )
    d_gates = jnp.sum(jnp.where(named, home.T[:, None, :], 0.0), axis=2)

    def outer(rows, columns):
        return lax.dot_general(
            rows, columns, (((0,), (0,)), ((), ())), preferred_element_type=jnp.float32
        )

    down_far = outer(gated[:, half:], all_u).astype(jnp.bfloat16)
    up_far = outer(all_x, d_hidden[:, half:]).astype(jnp.bfloat16)
    down_near = outer(gated[:, :half], all_u)
    up_near = outer(all_x, d_hidden[:, :half])
    grad_down = down_near + lax.ppermute(down_far, "tok", swap).astype(jnp.float32)
    grad_up = up_near + lax.ppermute(up_far, "tok", swap).astype(jnp.float32)
    return (
        mixed,
        d_tokens,
        d_gates,
        grad_up.astype(jnp.bfloat16)[None],
        grad_down.astype(jnp.bfloat16)[None],
    )


def shards(tokens, routes, gates, upstream, w_up, w_down):
    dense = 2 * routes.shape[1] >= lax.axis_size("expert") and lax.axis_size("tok") == 2
    body = dense_shards if dense else routed_shards
    return body(tokens, routes, gates, upstream, w_up, w_down)


def solution(mesh):
    return jax.shard_map(
        shards,
        mesh=mesh,
        in_specs=(
            P(("expert", "tok"), None),
            P(("expert", "tok"), None),
            P(("expert", "tok"), None),
            P(("expert", "tok"), None),
            P("expert", None, "tok"),
            P("expert", "tok", None),
        ),
        out_specs=(
            P(("expert", "tok"), None),
            P(("expert", "tok"), None),
            P(("expert", "tok"), None),
            P("expert", None, "tok"),
            P("expert", "tok", None),
        ),
        check_vma=False,
    )
```

```python
import jax
import jax.numpy as jnp
from jax import lax
from jax.sharding import PartitionSpec as P

GELU_C = 0.7978845608028654
GELU_A = 0.044715


def gelu_value(hidden):
    inner_arg = GELU_C * (hidden + GELU_A * hidden * hidden * hidden)
    return 0.5 * hidden * (1.0 + jnp.tanh(inner_arg))


def gelu_slope(hidden):
    tangent = jnp.tanh(GELU_C * (hidden + GELU_A * hidden * hidden * hidden))
    return 0.5 * (1.0 + tangent) + 0.5 * hidden * (1.0 - tangent * tangent) * GELU_C * (
        1.0 + 3.0 * GELU_A * hidden * hidden
    )


def expert_rows(rows_x, rows_grad, up_local, down_local):
    hidden = jnp.dot(rows_x, up_local, preferred_element_type=jnp.float32)
    active = gelu_value(hidden).astype(jnp.bfloat16)
    out_part = jnp.dot(active, down_local, preferred_element_type=jnp.float32)
    d_active = lax.dot_general(
        rows_grad, down_local, (((1,), (1,)), ((), ())), preferred_element_type=jnp.float32
    )
    d_hidden = (d_active * gelu_slope(hidden)).astype(jnp.bfloat16)
    dx_part = lax.dot_general(
        d_hidden, up_local, (((1,), (1,)), ((), ())), preferred_element_type=jnp.float32
    )
    grad_down = lax.dot_general(
        active, rows_grad, (((0,), (0,)), ((), ())), preferred_element_type=jnp.float32
    )
    grad_up = lax.dot_general(
        rows_x, d_hidden, (((0,), (0,)), ((), ())), preferred_element_type=jnp.float32
    )
    return (out_part, dx_part, grad_up, grad_down)


def routed_shards(tokens, routes, gates, upstream, w_up, w_down):
    tok_rows, feature_width = tokens.shape
    top_count = routes.shape[1]
    owners = lax.axis_size("expert")
    pair_count = lax.axis_size("tok")
    capacity = tok_rows * top_count // owners + max(1, tok_rows * top_count // (8 * owners))
    assigned = routes.reshape(-1)
    labels = jnp.arange(owners, dtype=jnp.int32)
    onehot = (assigned[:, None] == labels[None, :]).astype(jnp.int32)
    earlier = jnp.cumsum(onehot, axis=0) - onehot
    slot_rank = jnp.sum(earlier * onehot, axis=1)
    slot_of = assigned * capacity + slot_rank
    slot_ids = jnp.arange(owners * capacity, dtype=jnp.int32)
    matches = (slot_of[None, :] == slot_ids[:, None]).astype(jnp.int32)
    filled = jnp.sum(matches, axis=1) > 0
    source = jnp.sum(matches * jnp.arange(assigned.shape[0], dtype=jnp.int32)[None, :], axis=1)
    token_ids = source // top_count
    send_x = jnp.where(filled[:, None], tokens[token_ids], jnp.zeros((), jnp.bfloat16))
    gate_rows = jnp.where(filled, gates.reshape(-1)[source], jnp.zeros((), jnp.float32))
    send_grad = (gate_rows[:, None] * upstream[token_ids].astype(jnp.float32)).astype(jnp.bfloat16)
    send_x = send_x.reshape(owners, capacity, feature_width)
    send_grad = send_grad.reshape(owners, capacity, feature_width)
    recv_x, recv_grad = (
        lax.all_to_all(send_x, "expert", split_axis=0, concat_axis=0, tiled=True),
        lax.all_to_all(send_grad, "expert", split_axis=0, concat_axis=0, tiled=True),
    )
    both_x, both_grad = (
        lax.all_gather(recv_x[None], "tok", axis=0, tiled=True),
        lax.all_gather(recv_grad[None], "tok", axis=0, tiled=True),
    )
    rows_x = both_x.reshape(-1, feature_width)
    rows_grad = both_grad.reshape(-1, feature_width)
    out_part, dx_part, grad_up, grad_down = expert_rows(rows_x, rows_grad, w_up[0], w_down[0])
    shaped_out = out_part.reshape(pair_count, owners, capacity, feature_width)
    shaped_dx = dx_part.reshape(pair_count, owners, capacity, feature_width)
    summed_out, summed_dx = (
        lax.psum_scatter(shaped_out, "tok", scatter_dimension=0, tiled=True),
        lax.psum_scatter(shaped_dx, "tok", scatter_dimension=0, tiled=True),
    )
    home_out, home_dx = (
        lax.all_to_all(
            summed_out[0].astype(jnp.bfloat16), "expert", split_axis=0, concat_axis=0, tiled=True
        ),
        lax.all_to_all(
            summed_dx[0].astype(jnp.bfloat16), "expert", split_axis=0, concat_axis=0, tiled=True
        ),
    )
    out_pairs = (
        home_out.reshape(owners * capacity, feature_width)[slot_of]
        .reshape(tok_rows, top_count, feature_width)
        .astype(jnp.float32)
    )
    dx_pairs = (
        home_dx.reshape(owners * capacity, feature_width)[slot_of]
        .reshape(tok_rows, top_count, feature_width)
        .astype(jnp.float32)
    )
    mixed_out = jnp.sum(gates[:, :, None] * out_pairs, axis=1).astype(jnp.bfloat16)
    d_gates = jnp.sum(upstream.astype(jnp.float32)[:, None, :] * out_pairs, axis=2)
    d_tokens = jnp.sum(dx_pairs, axis=1).astype(jnp.bfloat16)
    return (
        mixed_out,
        d_tokens,
        d_gates,
        grad_up.astype(jnp.bfloat16)[None],
        grad_down.astype(jnp.bfloat16)[None],
    )


def swapped(array, bit):
    return lax.ppermute(array, "expert", tuple((i, i ^ bit) for i in range(16)))


def shifted(array, step, senders):
    return lax.ppermute(array, "expert", tuple((i, i + 4 * step) for z in senders for i in range(4 * z, 4 * z + 4)))


def add_rows(first, *others):
    total = first.astype(jnp.float32)
    for other in others:
        total = total + other.astype(jnp.float32)
    return total.astype(jnp.bfloat16)


def gathered_slots(block, layer, first, second):
    up_one = shifted(block, 1, (0, 1, 2))
    down_one = shifted(block, -1, (3, 2, 1))
    up_two = shifted(up_one, 1, (1, 2))
    down_two = shifted(down_one, -1, (2, 1))
    up_three = shifted(up_two, 1, (2,))
    down_three = shifted(down_two, -1, (1,))
    low = layer < 2
    far = jnp.where(low, jnp.where(layer == 0, down_three, up_one), jnp.where(layer == 3, up_three, down_one))
    columns = (block, jnp.where(low, down_one, up_one), jnp.where(low, down_two, up_two), far)
    slots = []
    for column in columns:
        pair = jnp.stack([column, swapped(column, first)])
        other = swapped(pair, second)
        if first == 1:
            slots.append(jnp.concatenate([pair[0], pair[1], other[0], other[1]], axis=0))
        else:
            slots.append(jnp.concatenate([pair[0], other[0], pair[1], other[1]], axis=0))
    return slots


def scattered_column(rows, tok_rows, first, second):
    blocks = [rows[i * tok_rows : (i + 1) * tok_rows].astype(jnp.bfloat16) for i in range(4)]
    kept, sent = ((0, 1), (2, 3)) if first == 2 else ((0, 2), (1, 3))
    came = swapped(jnp.stack([blocks[i] for i in sent]), first)
    near = add_rows(blocks[kept[0]], came[0])
    far = add_rows(blocks[kept[1]], came[1])
    return add_rows(near, swapped(far, second))


def scattered_layers(columns, layer):
    up = shifted(columns[3], 1, (0,))
    down = shifted(columns[3], -1, (3,))
    up = shifted(add_rows(columns[2], up), 1, (0, 1))
    down = shifted(add_rows(columns[2], down), -1, (3, 2))
    up = shifted(add_rows(jnp.where(layer == 2, columns[3], columns[1]), up), 1, (0, 1, 2))
    down = shifted(add_rows(jnp.where(layer == 1, columns[3], columns[1]), down), -1, (3, 2, 1))
    return add_rows(columns[0], up, down)


def transposed_dot(rows, weights):
    return lax.dot_general(
        rows, weights, (((1,), (1,)), ((), ())), preferred_element_type=jnp.float32
    )


def outer(rows, columns):
    return lax.dot_general(
        rows, columns, (((0,), (0,)), ((), ())), preferred_element_type=jnp.float32
    )


def dense_shards(tokens, routes, gates, upstream, w_up, w_down):
    tok_rows, width = tokens.shape
    owners = lax.axis_size("expert")
    half = w_up.shape[2]
    swap = ((0, 1), (1, 0))
    mine = lax.axis_index("expert")
    layer = mine // 4
    up_local, down_local = w_up[0], w_down[0]
    named = routes[:, :, None] == jnp.arange(owners, dtype=jnp.int32)
    gate_of = jnp.sum(jnp.where(named, gates[:, :, None], 0.0), axis=1)
    gate_all = lax.all_gather(gate_of, "expert", axis=0, tiled=True).reshape(owners, tok_rows, owners)
    gate_mine = lax.dynamic_index_in_dim(gate_all, mine, axis=2, keepdims=False)
    layers = (
        layer,
        jnp.where(layer < 2, layer + 1, layer - 1),
        jnp.where(layer < 2, layer + 2, layer - 2),
        jnp.where(layer % 2 == 0, 3, 0),
    )
    sources = [jnp.stack([z * 4 + (mine % 4 ^ flip) for flip in range(4)]) for z in layers]
    slots_x = gathered_slots(tokens, layer, 1, 2)
    slots_u = gathered_slots(upstream, layer, 2, 1)
    up_full = jnp.concatenate([up_local, lax.ppermute(up_local, "tok", swap)], axis=1)
    down_full = jnp.concatenate([down_local, lax.ppermute(down_local, "tok", swap)], axis=0)
    gated, slopes, inners = [None] * 4, [None] * 4, [None] * 4
    mixed_columns, dx_columns = [None] * 4, [None] * 4
    for s in range(4):
        gate = gate_mine[sources[s]].reshape(-1)[:, None]
        hidden = jnp.dot(slots_x[s], up_full, preferred_element_type=jnp.float32)
        value = gelu_value(hidden)
        gated[s] = (gate * value).astype(jnp.bfloat16)
        back = transposed_dot(slots_u[s], down_full)
        inners[s] = jnp.sum(value * back, axis=1).reshape(4, tok_rows)
        slopes[s] = (gate * back * gelu_slope(hidden)).astype(jnp.bfloat16)
    for s in (3, 2, 1, 0):
        out_part = jnp.dot(gated[s], down_full, preferred_element_type=jnp.float32)
        mixed_columns[s] = scattered_column(out_part, tok_rows, 2, 1)
        dx_part = transposed_dot(slopes[s], up_full)
        dx_columns[s] = scattered_column(dx_part, tok_rows, 1, 2)
    mixed = scattered_layers(mixed_columns, layer)
    d_tokens = scattered_layers(dx_columns, layer)

    order = jnp.concatenate(sources)
    inner = jnp.zeros((owners, tok_rows), jnp.float32).at[order].set(jnp.concatenate(inners))
    inner_all = lax.all_gather(inner, "expert", axis=0, tiled=True).reshape(owners, owners, tok_rows)
    home = lax.dynamic_index_in_dim(inner_all, mine, axis=1, keepdims=False)
    d_gates = jnp.sum(jnp.where(named, home.T[:, None, :], 0.0), axis=2)

    all_x, all_u = jnp.concatenate(slots_x), jnp.concatenate(slots_u)
    act, d_hidden = jnp.concatenate(gated), jnp.concatenate(slopes)
    down_far = outer(act[:, half:], all_u).astype(jnp.bfloat16)
    up_far = outer(all_x, d_hidden[:, half:]).astype(jnp.bfloat16)
    down_near = outer(act[:, :half], all_u)
    up_near = outer(all_x, d_hidden[:, :half])
    grad_down = down_near + lax.ppermute(down_far, "tok", swap).astype(jnp.float32)
    grad_up = up_near + lax.ppermute(up_far, "tok", swap).astype(jnp.float32)
    return (
        mixed,
        d_tokens,
        d_gates,
        grad_up.astype(jnp.bfloat16)[None],
        grad_down.astype(jnp.bfloat16)[None],
    )


def shards(tokens, routes, gates, upstream, w_up, w_down):
    dense = lax.axis_size("expert") == 16 and lax.axis_size("tok") == 2
    body = dense_shards if dense else routed_shards
    return body(tokens, routes, gates, upstream, w_up, w_down)


def solution(mesh):
    return jax.shard_map(
        shards,
        mesh=mesh,
        in_specs=(
            P(("expert", "tok"), None),
            P(("expert", "tok"), None),
            P(("expert", "tok"), None),
            P(("expert", "tok"), None),
            P("expert", None, "tok"),
            P("expert", "tok", None),
        ),
        out_specs=(
            P(("expert", "tok"), None),
            P(("expert", "tok"), None),
            P(("expert", "tok"), None),
            P("expert", None, "tok"),
            P("expert", "tok", None),
        ),
        check_vma=False,
    )
```
